32 devices in a mesh: dp: 4 (over z), expert: 8 (over y, x, core).
Axes of the slice: x: 2, y: 2, z: 4, core: 2. Of those that a mesh axis runs over, the one named last changes fastest.
Arguments:
- tokens: bfloat16 [2, 64, 197, 768], P(None, ('dp', 'expert')), may hold values from -6 to 6
- image_count: int32 [2, 32], P(None, ('dp', 'expert')), may hold values from 1 to 2, 48 in all within a row
- adapter_index: int32 [2, 64], P(None, ('dp', 'expert')), may hold values from 0 to 7
- expert_ids: int32 [2, 64, 197, 2], P(None, ('dp', 'expert')), may hold values from 0 to 7, as said below
- norm_gains: bfloat16 [2, 768], P(None, ('dp', 'expert')), may hold values from 0.25 to 1.75
- attention_in: bfloat16 [768, 2304], P(('dp', 'expert')), may hold values from -0.21875 to 0.21875
- attention_out: bfloat16 [768, 768], P(('dp', 'expert')), may hold values from -0.625 to 0.625
- router: bfloat16 [768, 8], P(('dp', 'expert')), may hold values from -0.14941406 to 0.14941406
- expert_in: bfloat16 [8, 768, 3072], P('expert', 'dp'), may hold values from -0.21875 to 0.21875
- expert_out: bfloat16 [8, 3072, 768], P('expert', 'dp'), may hold values from -0.109375 to 0.109375
- attention_down: bfloat16 [768, 4, 8, 16], P(('dp', 'expert')), may hold values from -0.21875 to 0.21875
- attention_up: bfloat16 [4, 8, 16, 768], P(None, None, None, ('dp', 'expert')), may hold values from -0.75 to 0.75
- expert_down_in: bfloat16 [8, 768, 8, 16], P('expert', 'dp'), may hold values from -0.21875 to 0.21875
- expert_up_in: bfloat16 [8, 8, 16, 3072], P('expert', None, None, 'dp'), may hold values from -0.75 to 0.75
- expert_down_out: bfloat16 [8, 3072, 8, 16], P('expert', 'dp'), may hold values from -0.15625 to 0.15625
- expert_up_out: bfloat16 [8, 8, 16, 768], P('expert', None, None, 'dp'), may hold values from -0.75 to 0.75
- cotangent: bfloat16 [2, 64, 197, 768], P(None, ('dp', 'expert')), may hold values from -6 to 6
Outputs:
- output: bfloat16 [2, 64, 197, 768], P(None, ('dp', 'expert'))
- input_grad: bfloat16 [2, 64, 197, 768], P(None, ('dp', 'expert'))
- attention_down_grad: float32 [768, 4, 8, 16], P(('dp', 'expert'))
- attention_up_grad: float32 [4, 8, 16, 768], P(None, None, None, ('dp', 'expert'))
- expert_down_in_grad: float32 [8, 768, 8, 16], P('expert', 'dp')
- expert_up_in_grad: float32 [8, 8, 16, 3072], P('expert', None, None, 'dp')
- expert_down_out_grad: float32 [8, 3072, 8, 16], P('expert', 'dp')
- expert_up_out_grad: float32 [8, 8, 16, 768], P('expert', None, None, 'dp')
The draws below stay inside these ranges and needn't reach their ends.
Inputs may be any that keep to these rules, and one draw needn't show every extreme that they name: The first image_count[m, d] of the 2 image slots of device d in micro-batch m are live; each micro-batch's counts sum to 48. `expert_ids`: the two experts of a token differ. Among the 394 tokens of one device in one micro-batch (its 2 consecutive image slots), live or not, no expert is named more than 110 times, and in every such block some expert is named exactly 110 times.
All inputs are finite; a program needn't handle non-finite values.
Results may differ from the reference program's by a relative error of at most 0.017.
Values may be sent and summed in bfloat16 or wider, within the bound.
No kernel may reach another device: no remote copies, remote signals or barrier semaphores. Data moves between devices by JAX's collectives and lax.ppermute only.
A program may use at most 256 MiB of HBM per device.

```python
import math
from functools import partial
import jax
import jax.numpy as jnp
import numpy as np
from jax import lax

D = 768
HEAD_DIM = 64
FF = 3072
SEQ = 197
RANK = 16
ADAPTERS = 8
MICRO = 2
IMG_SLOT = 2
EXPERTS = 8
IMAGES = 64
HOT = 55
CAP = 110
DEVICES = 32


def route_block(block_key):
    rows = IMG_SLOT * SEQ
    first_key, second_key, third_key = jax.random.split(block_key, 3)
    favoured = jax.random.randint(first_key, (), 0, EXPERTS, dtype=jnp.int32)
    tickets = jnp.arange((EXPERTS - 1) * HOT, dtype=jnp.int32) // HOT
    others = (tickets + favoured + 1) % EXPERTS
    others = jax.random.permutation(second_key, others)
    chosen = jnp.concatenate([jnp.full((HOT,), favoured, dtype=jnp.int32), others[:rows - HOT]])
    ordered = jnp.sort(chosen)
    partner = jnp.roll(ordered, -(rows // 2))
    paired = jnp.stack([ordered, partner], axis=1)
    order = jax.random.permutation(third_key, rows)
    return paired[order]


def draw_expert_ids(key, part):
    devices = IMAGES // IMG_SLOT
    block_keys = jax.random.split(key, MICRO * devices)
    routes = jax.vmap(route_block)(block_keys)
    return routes.reshape(MICRO, IMAGES, SEQ, 2).astype(jnp.int32)


def with_ends(entries, rng, low, largest):
    spot = [jax.random.randint(jax.random.fold_in(rng, axis), (), 0, length) for axis, length in enumerate(entries.shape)]
    widest = entries.shape.index(max(entries.shape))
    next_to = spot[:widest] + [(spot[widest] + 1) % entries.shape[widest]] + spot[widest + 1:]
    return entries.at[tuple(spot)].set(low).at[tuple(next_to)].set(largest)


def steps_of(key, shape, pieces, least, high):
    def one(axis_at, shards_of):
        steps = jax.random.uniform(jax.random.fold_in(jax.random.fold_in(key, 6), axis_at), (shards_of,), jnp.float32, least / len(pieces), high / len(pieces))
        return jnp.repeat(jnp.exp(steps), shape[axis_at] // shards_of).reshape((-1,) + (1,) * (len(shape) - axis_at - 1))

    factor_of = one(*pieces[0])
    for cut in pieces[1:]:
        factor_of = factor_of * one(*cut)
    return factor_of


def length_profile(number_of, total, most, slope):
    portions = [(1 << 20) // math.isqrt(standing ** slope) + 1 for standing in range(2, number_of + 1)]
    spare, given = total - most - (number_of - 1), [1] * (number_of - 1)
    while spare > 0:
        candidates = [i for i in range(number_of - 1) if given[i] < most]
        mass, budget = sum([portions[i] for i in candidates]), spare
        for i in candidates:
            addition = min(most - given[i], max(1, budget * portions[i] // mass), spare)
            given[i] = given[i] + addition
            spare = spare - addition
    return np.array([most] + given)


def ragged(rng, number_of, total, reach, skew):
    if number_of == 2:
        one = jax.random.randint(rng, (), max(1, total - reach), min(reach, total - 1) + 1)
        return jnp.stack([one, total - one])
    lengths = jnp.asarray(length_profile(number_of, total, reach, skew), jnp.int32)
    pairs = (number_of - 1) // 2
    source_of, receiver = lengths[1:1 + 2 * pairs:2], lengths[2:2 + 2 * pairs:2]
    room = jnp.minimum(source_of - 1, reach - receiver)
    passed = jax.random.randint(jax.random.fold_in(rng, 1), (pairs,), 0, 1 << 20) % (room + 1)
    lengths = lengths.at[1:1 + 2 * pairs:2].set(source_of - passed).at[2:2 + 2 * pairs:2].set(receiver + passed)
    return lengths[jax.random.permutation(jax.random.fold_in(rng, 2), number_of)]


def normal_values(key, dims, scale, limit, shards=(), kind=jnp.bfloat16):
    values = scale * jax.random.normal(key, dims, jnp.float32)
    if shards:
        values = values * steps_of(key, dims, shards, -0.22, 0.18)
    return jnp.clip(values, -limit, limit).astype(kind)


def setup_inputs(seed: int = 0) -> dict:
    arg_keys = jax.random.split(jax.random.key(seed), 18)
    return {
        "tokens": normal_values(arg_keys[0], (MICRO, IMAGES, SEQ, D), 1.0, 6.0, ((1, 32),)),
        "image_count": jax.vmap(lambda own: ragged(own, DEVICES, (3 * IMG_SLOT * DEVICES) // 4, IMG_SLOT, 0))(jax.random.split(arg_keys[1], MICRO)).reshape((MICRO, DEVICES)).astype(jnp.int32),
        "adapter_index": with_ends(jax.random.randint(arg_keys[2], (MICRO, IMAGES), 0, ADAPTERS), jax.random.fold_in(arg_keys[2], 1), 0, ADAPTERS - 1).astype(jnp.int32),
        "expert_ids": draw_expert_ids(jax.random.fold_in(arg_keys[17], 71), 0),
        "norm_gains": jnp.clip(1.0 + 0.15 * jax.random.normal(arg_keys[4], (2, D), jnp.float32), 0.25, 1.75).astype(jnp.bfloat16),
        "attention_in": normal_values(arg_keys[5], (D, 3 * D), D ** -0.5, 0.21875, ((0, 32),)),
        "attention_out": normal_values(arg_keys[6], (D, D), (D // 8) ** -0.5, 0.625, ((0, 32),)),
        "router": normal_values(arg_keys[7], (D, EXPERTS), 0.025, 0.14941406, ((0, 32),)),
        "expert_in": normal_values(arg_keys[8], (EXPERTS, D, FF), D ** -0.5, 0.21875, ((0, 8), (1, 4))),
        "expert_out": normal_values(arg_keys[9], (EXPERTS, FF, D), FF ** -0.5, 0.109375, ((0, 8), (1, 4))),
        "attention_down": normal_values(arg_keys[10], (D, 4, ADAPTERS, RANK), D ** -0.5, 0.21875, ((0, 32),)),
        "attention_up": normal_values(arg_keys[11], (4, ADAPTERS, RANK, D), 0.125, 0.75, ((3, 32),)),
        "expert_down_in": normal_values(arg_keys[12], (EXPERTS, D, ADAPTERS, RANK), D ** -0.5, 0.21875, ((0, 8), (1, 4))),
        "expert_up_in": normal_values(arg_keys[13], (EXPERTS, ADAPTERS, RANK, FF), 0.125, 0.75, ((0, 8), (3, 4))),
        "expert_down_out": normal_values(arg_keys[14], (EXPERTS, FF, ADAPTERS, RANK), (FF // 2) ** -0.5, 0.15625, ((0, 8), (1, 4))),
        "expert_up_out": normal_values(arg_keys[15], (EXPERTS, ADAPTERS, RANK, D), 0.125, 0.75, ((0, 8), (3, 4))),
        "cotangent": normal_values(arg_keys[16], (MICRO, IMAGES, SEQ, D), 1.0, 6.0, ((1, 32),)),
    }


@jax.custom_vjp
def low(v):
    return lax.optimization_barrier(v.astype(jnp.bfloat16)).astype(jnp.float32)

@jax.custom_vjp
def low_back(v):
    return v

def low_keep(v):
    return (low(v), None)

def low_pass(kept, grad):
    return (grad,)

def back_keep(v):
    return (v, None)

def back_low(kept, grad):
    return (low(grad),)
low.defvjp(low_keep, low_pass)
low_back.defvjp(back_keep, back_low)
HIGHEST = lax.Precision.HIGHEST

def layer_norm(inputs, scale_row):
    average = lax.optimization_barrier(jnp.mean(inputs, axis=-1, keepdims=True))
    centred = inputs - average
    spread = lax.optimization_barrier(jnp.mean(centred * centred, axis=-1, keepdims=True))
    return centred * lax.rsqrt(spread + 1e-06) * scale_row

def attend_block(frozen, adapters, inputs, adapt, count, routes):
    norm_gains, attention_in, attention_out, router, expert_in, expert_out = frozen
    attention_down, attention_up, expert_down_in, expert_up_in, expert_down_out, expert_up_out = adapters
    images, length, width = inputs.shape
    heads = width // HEAD_DIM
    rows = images * length
    experts = router.shape[1]
    factor = 1.0 / math.sqrt(HEAD_DIM)
    normed = low(layer_norm(inputs, norm_gains[0]))
    chosen_down = jnp.take(attention_down, adapt, axis=2)
    chosen_up = jnp.take(attention_up, adapt, axis=1)
    narrow = low(low_back(jnp.einsum('isd,djir->isjr', normed, chosen_down[:, :3], precision=HIGHEST)))
    widened = jnp.einsum('isjr,jird->isjd', narrow, chosen_up[:3], precision=HIGHEST)
    projected = jnp.einsum('isd,de->ise', normed, attention_in, precision=HIGHEST).reshape(images, length, 3, width)
    projected = low(low_back(projected + widened))
    queries = projected[:, :, 0].reshape(images, length, heads, HEAD_DIM)
    keys = projected[:, :, 1].reshape(images, length, heads, HEAD_DIM)
    values = projected[:, :, 2].reshape(images, length, heads, HEAD_DIM)
    scores = low_back(jnp.einsum('ishc,ithc->ihst', queries, keys, precision=HIGHEST) * factor)
    weights = low(jax.nn.softmax(scores, axis=-1))
    mixed = jnp.einsum('ihst,ithc->ishc', weights, values, precision=HIGHEST).reshape(images, length, width)
    mixed = low(low_back(mixed))
    narrow_out = low(low_back(jnp.einsum('isd,dir->isr', mixed, chosen_down[:, 3], precision=HIGHEST)))
    branch = jnp.einsum('isd,de->ise', mixed, attention_out, precision=HIGHEST) + jnp.einsum('isr,ird->isd', narrow_out, chosen_up[3], precision=HIGHEST)
    hidden = inputs + low_back(branch)
    flat = low(layer_norm(hidden, norm_gains[1])).reshape(rows, width)
    picks = routes.reshape(rows, 2)
    logits = jnp.dot(flat, router, precision=HIGHEST)
    gates = jax.nn.softmax(jnp.take_along_axis(logits, picks, axis=1), axis=-1)
    flat_picks = picks.reshape(-1)
    hits = (flat_picks[:, None] == jnp.arange(experts, dtype=jnp.int32)[None, :]).astype(jnp.int32)
    placed = lax.optimization_barrier(jnp.sum((jnp.cumsum(hits, axis=0) - 1) * hits, axis=1))
    slots = (flat_picks * CAP + placed).astype(jnp.int32)
    owners = jnp.arange(2 * rows, dtype=jnp.int32) // 2
    source = jnp.zeros((experts * CAP,), jnp.int32).at[slots].set(owners)
    slot_adapt = jnp.repeat(adapt, length)[source].reshape(experts, CAP)
    mask = (slot_adapt[:, :, None] == jnp.arange(ADAPTERS, dtype=jnp.int32)[None, None, :]).astype(jnp.float32)[..., None]
    sent = low_back(flat[source]).reshape(experts, CAP, width)
    thin_in = low(low_back(jnp.einsum('ecd,edar->ecar', sent, expert_down_in, precision=HIGHEST) * mask))
    lifted = jnp.einsum('ecd,edf->ecf', sent, expert_in, precision=HIGHEST) + jnp.einsum('ecar,earf->ecf', thin_in, expert_up_in, precision=HIGHEST)
    lifted = low_back(lifted)
    active = low(jax.nn.gelu(lifted, approximate=False))
    thin_out = low(low_back(jnp.einsum('ecf,efar->ecar', active, expert_down_out, precision=HIGHEST) * mask))
    result = jnp.einsum('ecf,efd->ecd', active, expert_out, precision=HIGHEST) + jnp.einsum('ecar,eard->ecd', thin_out, expert_up_out, precision=HIGHEST)
    result = low(low_back(result))
    returned = result.reshape(experts * CAP, width)[slots].reshape(rows, 2, width)
    mixture = lax.optimization_barrier(jnp.sum(gates[:, :, None] * returned, axis=1)).reshape(images, length, width)
    living = (jnp.arange(images, dtype=jnp.int32) < count).astype(jnp.float32)
    return (hidden + mixture) * living[:, None, None]

def reference(tokens, image_count, adapter_index, expert_ids, norm_gains, attention_in, attention_out, router, expert_in, expert_out, attention_down, attention_up, expert_down_in, expert_up_in, expert_down_out, expert_up_out, cotangent):
    frozen = tuple((array.astype(jnp.float32) for array in (norm_gains, attention_in, attention_out, router, expert_in, expert_out)))
    adapters = tuple((array.astype(jnp.float32) for array in (attention_down, attention_up, expert_down_in, expert_up_in, expert_down_out, expert_up_out)))
    micro, images, length, width = tokens.shape
    devices = image_count.shape[1]
    blocks = micro * devices
    group = math.gcd(8, blocks)
    layout = (blocks // group, group)
    inputs = tokens.astype(jnp.float32).reshape(layout + (IMG_SLOT, length, width))
    adapt = adapter_index.reshape(layout + (IMG_SLOT,))
    counts = image_count.reshape(layout)
    routes = expert_ids.reshape(layout + (IMG_SLOT, length, 2))

    def forward(inputs, adapters):

        def one_group(pack):
            group_inputs, group_adapt, group_counts, group_routes = pack
            return jax.vmap(partial(attend_block, frozen, adapters))(group_inputs, group_adapt, group_counts, group_routes)
        return lax.map(jax.checkpoint(one_group), (inputs, adapt, counts, routes))
    output, pullback = jax.vjp(forward, inputs, adapters)
    input_grad, adapter_grads = pullback(cotangent.astype(jnp.float32).reshape(inputs.shape))
    shape = tokens.shape
    return (output.reshape(shape).astype(jnp.bfloat16), input_grad.reshape(shape).astype(jnp.bfloat16), adapter_grads[0], adapter_grads[1], adapter_grads[2], adapter_grads[3], adapter_grads[4], adapter_grads[5])
```

```python
import functools
import math

import jax
import jax.numpy as jnp
from jax import lax
from jax.experimental import pallas as pl
from jax.experimental.pallas import tpu as pltpu
from jax.sharding import PartitionSpec as P

HEAD_DIM = 64
RANK = 16
ADAPTERS = 8
NARROW = ADAPTERS * RANK
LANES = 128
EPSILON = 1e-06
BF16 = jnp.bfloat16
F32 = jnp.float32
VMEM_LIMIT = 60 * 1024 * 1024


def mm(left, right):
    return lax.dot_general(left, right, (((1,), (0,)), ((), ())), preferred_element_type=F32)


def mm_nt(left, right):
    return lax.dot_general(left, right, (((1,), (1,)), ((), ())), preferred_element_type=F32)


def mm_tn(left, right):
    return lax.dot_general(left, right, (((0,), (0,)), ((), ())), preferred_element_type=F32)


def normal_of(value):
    average = jnp.mean(value, axis=-1, keepdims=True)
    centred = value - average
    spread = jnp.mean(centred * centred, axis=-1, keepdims=True)
    inverse = lax.rsqrt(spread + EPSILON)
    return centred * inverse, inverse


def norm_back(grad_norm, normal, inverse, scale_row):
    scaled = grad_norm * scale_row
    first = jnp.mean(scaled, axis=-1, keepdims=True)
    second = jnp.mean(scaled * normal, axis=-1, keepdims=True)
    return inverse * (scaled - first - normal * second)


def capacity_of(rows, experts):
    return 2 * max(1, 9 * rows // (8 * experts))


def lane_adapter(shape):
    return lax.broadcasted_iota(jnp.int32, shape, len(shape) - 1) % NARROW // RANK


def attention_forward_kernel(
    adapt_ref, x_ref, a_ref, b_ref, gains_ref, slots_ref,
    qkv_ref, weights_ref, mixed_ref, narrow_ref, hidden_ref, send_ref,
):
    step = pl.program_id(0)
    width = x_ref.shape[2]
    heads = width // HEAD_DIM
    x = x_ref[0].astype(F32)
    length = x.shape[0]
    normal, _ = normal_of(x)
    normed = (normal * gains_ref[0:1, :]).astype(BF16)
    adapter = adapt_ref[step]
    down_at = 2 * width
    mask = (lane_adapter((1, 3 * NARROW)) == adapter).astype(F32)
    narrow = (mm(normed, a_ref[:, down_at : down_at + 3 * NARROW]) * mask).astype(BF16)
    narrow_ref[0, :, : 3 * NARROW] = narrow
    for part in range(3):
        matrix = (a_ref[:, :width], a_ref[:, width : 2 * width], b_ref[:, :width])[part]
        up_at = 2 * width + part * NARROW
        block = mm(normed, matrix) + mm_nt(
            narrow[:, part * NARROW : (part + 1) * NARROW], b_ref[:, up_at : up_at + NARROW]
        )
        qkv_ref[0, :, part * width : (part + 1) * width] = block.astype(BF16)
    low_half = lax.broadcasted_iota(jnp.int32, (length, LANES), 1) < HEAD_DIM
    factor = 1.0 / math.sqrt(HEAD_DIM)
    for pair in range(heads // 2):
        at = pair * LANES
        queries = qkv_ref[0, :, at : at + LANES]
        keys = qkv_ref[0, :, width + at : width + at + LANES]
        values = qkv_ref[0, :, 2 * width + at : 2 * width + at + LANES]
        halves = []
        for half in range(2):
            own = low_half if half == 0 else jnp.logical_not(low_half)
            masked = jnp.where(own, queries, jnp.zeros_like(queries))
            scores = mm_nt(masked, keys) * factor
            peak = jnp.max(scores, axis=-1, keepdims=True)
            exponent = jnp.exp(scores - peak)
            total = jnp.sum(exponent, axis=-1, keepdims=True)
            weights = (exponent * (1.0 / total)).astype(BF16)
            weights_ref[0, 2 * pair + half] = weights
            halves.append(mm(weights, values))
        mixed_ref[0, :, at : at + LANES] = jnp.where(low_half, halves[0], halves[1]).astype(BF16)
    mixed = mixed_ref[0]
    out_mask = mask[:, :NARROW]
    narrow_out = (mm(mixed, a_ref[:, down_at + 3 * NARROW : down_at + 4 * NARROW]) * out_mask).astype(BF16)
    narrow_ref[0, :, 3 * NARROW :] = narrow_out
    up_at = 2 * width + 3 * NARROW
    hidden = x + (mm(mixed, b_ref[:, width : 2 * width]) + mm_nt(narrow_out, b_ref[:, up_at : up_at + NARROW]))
    hidden_ref[0] = hidden
    second, _ = normal_of(hidden)
    flat = (second * gains_ref[1:2, :]).astype(BF16)
    slot_ids = lax.broadcasted_iota(jnp.int32, (send_ref.shape[0] * send_ref.shape[1], length), 0)
    hit = jnp.logical_or(slot_ids == slots_ref[0, 0:1, :], slot_ids == slots_ref[0, 1:2, :])
    sent = mm(hit.astype(F32).astype(BF16), flat).astype(BF16).reshape(send_ref.shape)

    @pl.when(step == 0)
    def _():
        send_ref[...] = sent

    @pl.when(step > 0)
    def _():
        send_ref[...] = send_ref[...] + sent


def attention_forward(micro, adapt, x4, side_a, side_b, gains, slots_row, experts, padded):
    images = adapt.shape[0]
    _, length, width = x4.shape
    heads = width // HEAD_DIM
    first = micro * images
    whole = lambda array: pl.BlockSpec(array.shape, lambda i, *_: (0,) * array.ndim)
    image = lambda *dims: pl.BlockSpec((1,) + dims, lambda i, *_: (i,) + (0,) * len(dims))
    return pl.pallas_call(
        attention_forward_kernel,
        grid_spec=pltpu.PrefetchScalarGridSpec(
            num_scalar_prefetch=1,
            grid=(images,),
            in_specs=[
                pl.BlockSpec((1, length, width), lambda i, *_: (first + i, 0, 0)),
                whole(side_a),
                whole(side_b),
                whole(gains),
                pl.BlockSpec((1, 2, length), lambda i, *_: (first + i, 0, 0)),
            ],
            out_specs=[
                image(length, 3 * width),
                image(heads, length, length),
                image(length, width),
                image(length, 4 * NARROW),
                image(length, width),
                pl.BlockSpec((experts, padded, width), lambda i, *_: (0, 0, 0)),
            ],
        ),
        out_shape=[
            jax.ShapeDtypeStruct((images, length, 3 * width), BF16),
            jax.ShapeDtypeStruct((images, heads, length, length), BF16),
            jax.ShapeDtypeStruct((images, length, width), BF16),
            jax.ShapeDtypeStruct((images, length, 4 * NARROW), BF16),
            jax.ShapeDtypeStruct((images, length, width), F32),
            jax.ShapeDtypeStruct((experts, padded, width), BF16),
        ],
        compiler_params=pltpu.CompilerParams(vmem_limit_bytes=VMEM_LIMIT),
        name="attention_forward",
    )(adapt, x4, side_a, side_b, gains, slots_row)


def attention_backward_kernel(
    adapt_ref, count_ref, x_ref, cot_ref, a_ref, b_ref, gains_ref, slots_ref,
    qkv_ref, weights_ref, mixed_ref, narrow_ref, hidden_ref, home_ref,
    grad_ref, down_grad_ref, up_grad_ref, grad_qkv_ref, grad_mixed_ref,
):
    step = pl.program_id(0)
    width = x_ref.shape[2]
    heads = width // HEAD_DIM
    x = x_ref[0].astype(F32)
    length = x.shape[0]
    adapter = adapt_ref[step]
    live = jnp.where(step < count_ref[0], 1.0, 0.0).astype(F32)
    factor = 1.0 / math.sqrt(HEAD_DIM)
    mask = (lane_adapter((1, 3 * NARROW)) == adapter).astype(F32)
    out_mask = mask[:, :NARROW]
    down_at = 2 * width

    delta = cot_ref[0].astype(F32) * live
    slots = home_ref.shape[0] * home_ref.shape[1]
    slot_ids = lax.broadcasted_iota(jnp.int32, (length, slots), 1)
    hit = jnp.logical_or(slot_ids == slots_ref[0, :, 0:1], slot_ids == slots_ref[0, :, 1:2])
    grad_flat = mm(hit.astype(F32).astype(BF16), home_ref[...].reshape(slots, width))
    second, second_inverse = normal_of(hidden_ref[0])
    grad_hidden = delta + norm_back(grad_flat, second, second_inverse, gains_ref[1:2, :])
    branch = grad_hidden.astype(BF16)
    up_at = 2 * width + 3 * NARROW
    grad_narrow_out = (mm(branch, b_ref[:, up_at : up_at + NARROW]) * out_mask).astype(BF16)
    grad_mixed_ref[...] = (
        mm_nt(branch, b_ref[:, width : 2 * width])
        + mm_nt(grad_narrow_out, a_ref[:, down_at + 3 * NARROW : down_at + 4 * NARROW])
    ).astype(BF16)
    low_half = lax.broadcasted_iota(jnp.int32, (length, LANES), 1) < HEAD_DIM
    for pair in range(heads // 2):
        at = pair * LANES
        queries = qkv_ref[0, :, at : at + LANES]
        keys = qkv_ref[0, :, width + at : width + at + LANES]
        values = qkv_ref[0, :, 2 * width + at : 2 * width + at + LANES]
        mixed_grad = grad_mixed_ref[:, at : at + LANES]
        parts = []
        for half in range(2):
            own = low_half if half == 0 else jnp.logical_not(low_half)
            masked = jnp.where(own, mixed_grad, jnp.zeros_like(mixed_grad))
            weights = weights_ref[0, 2 * pair + half]
            probs = weights.astype(F32)
            grad_probs = mm_nt(masked, values)
            inner = jnp.sum(probs * grad_probs, axis=-1, keepdims=True)
            grad_scores = (probs * (grad_probs - inner)).astype(BF16)
            parts.append(
                (mm(grad_scores, keys), mm_tn(grad_scores, queries), mm_tn(weights, mixed_grad))
            )
        for part in range(3):
            merged = jnp.where(low_half, parts[0][part], parts[1][part])
            if part < 2:
                merged = merged * factor
            grad_qkv_ref[:, part * width + at : part * width + at + LANES] = merged.astype(BF16)
    normal, inverse = normal_of(x)
    normed = (normal * gains_ref[0:1, :]).astype(BF16)
    mixed = mixed_ref[0]
    grad_normed = None
    for part in range(3):
        block = grad_qkv_ref[:, part * width : (part + 1) * width]
        matrix = (a_ref[:, :width], a_ref[:, width : 2 * width], b_ref[:, :width])[part]
        up_at = 2 * width + part * NARROW
        narrow_mask = mask[:, :NARROW]
        grad_narrow = (mm(block, b_ref[:, up_at : up_at + NARROW]) * narrow_mask).astype(BF16)
        down_part = down_at + part * NARROW
        term = mm_nt(block, matrix) + mm_nt(grad_narrow, a_ref[:, down_part : down_part + NARROW])
        grad_normed = term if grad_normed is None else grad_normed + term
        down_new = mm_tn(normed, grad_narrow)
        up_new = mm_tn(block, narrow_ref[0, :, part * NARROW : (part + 1) * NARROW])
        cols = slice(part * NARROW, (part + 1) * NARROW)

        @pl.when(step == 0)
        def _(cols=cols, down_new=down_new, up_new=up_new):
            down_grad_ref[:, cols] = down_new
            up_grad_ref[:, cols] = up_new

        @pl.when(step > 0)
        def _(cols=cols, down_new=down_new, up_new=up_new):
            down_grad_ref[:, cols] = down_grad_ref[:, cols] + down_new
            up_grad_ref[:, cols] = up_grad_ref[:, cols] + up_new

    cols = slice(3 * NARROW, 4 * NARROW)
    down_new = mm_tn(mixed, grad_narrow_out)
    up_new = mm_tn(branch, narrow_ref[0, :, 3 * NARROW :])

    @pl.when(step == 0)
    def _():
        down_grad_ref[:, cols] = down_new
        up_grad_ref[:, cols] = up_new

    @pl.when(step > 0)
    def _():
        down_grad_ref[:, cols] = down_grad_ref[:, cols] + down_new
        up_grad_ref[:, cols] = up_grad_ref[:, cols] + up_new

    grad_ref[0] = (grad_hidden + norm_back(grad_normed, normal, inverse, gains_ref[0:1, :])).astype(BF16)


def attention_backward(micro, adapt, count, x4, cot4, side_a, side_b, gains, slots_col, kept, home):
    qkv, weights, mixed, narrow, hidden = kept
    images = adapt.shape[0]
    _, length, width = x4.shape
    heads = width // HEAD_DIM
    first = micro * images
    whole = lambda array: pl.BlockSpec(array.shape, lambda i, *_: (0,) * array.ndim)
    image = lambda *dims: pl.BlockSpec((1,) + dims, lambda i, *_: (i,) + (0,) * len(dims))
    return pl.pallas_call(
        attention_backward_kernel,
        grid_spec=pltpu.PrefetchScalarGridSpec(
            num_scalar_prefetch=2,
            grid=(images,),
            in_specs=[
                pl.BlockSpec((1, length, width), lambda i, *_: (first + i, 0, 0)),
                pl.BlockSpec((1, length, width), lambda i, *_: (first + i, 0, 0)),
                whole(side_a),
                whole(side_b),
                whole(gains),
                pl.BlockSpec((1, length, 2), lambda i, *_: (first + i, 0, 0)),
                image(length, 3 * width),
                image(heads, length, length),
                image(length, width),
                image(length, 4 * NARROW),
                image(length, width),
                whole(home),
            ],
            out_specs=[
                image(length, width),
                pl.BlockSpec((width, 4 * NARROW), lambda i, *_: (0, 0)),
                pl.BlockSpec((width, 4 * NARROW), lambda i, *_: (0, 0)),
            ],
            scratch_shapes=[pltpu.VMEM((length, 3 * width), BF16), pltpu.VMEM((length, width), BF16)],
        ),
        out_shape=[
            jax.ShapeDtypeStruct((images, length, width), BF16),
            jax.ShapeDtypeStruct((width, 4 * NARROW), F32),
            jax.ShapeDtypeStruct((width, 4 * NARROW), F32),
        ],
        compiler_params=pltpu.CompilerParams(vmem_limit_bytes=VMEM_LIMIT),
        name="attention_backward",
    )(adapt, count, x4, cot4, side_a, side_b, gains, slots_col, qkv, weights, mixed, narrow, hidden, home)


def dispatch_kernel(count_ref, cot_ref, slots_ref, meta_ref, out_ref):
    micro = pl.program_id(0)
    images, length, width = cot_ref.shape
    experts, padded, _ = out_ref.shape
    slot_ids = lax.broadcasted_iota(jnp.int32, (experts * padded, length), 0)
    rows = None
    meta = None
    for image in range(images):
        hits = [(slot_ids == slots_ref[image, k : k + 1, :]).astype(F32).astype(BF16) for k in range(2)]
        live = jnp.where(image < count_ref[micro], 1.0, 0.0).astype(F32)
        delta = (cot_ref[image].astype(F32) * live).astype(BF16)
        term = mm(hits[0] + hits[1], delta)
        extra = mm(hits[0], meta_ref[image, 0]) + mm(hits[1], meta_ref[image, 1])
        rows = term if rows is None else rows + term
        meta = extra if meta is None else meta + extra
    out_ref[:, :, :width] = rows.astype(BF16).reshape(experts, padded, width)
    out_ref[:, :, width:] = meta.astype(BF16).reshape(experts, padded, LANES)


def dispatch(counts, cot4, slots_row, meta, experts, padded):
    micros = counts.shape[0]
    total, length, width = cot4.shape
    images = total // micros
    return pl.pallas_call(
        dispatch_kernel,
        grid_spec=pltpu.PrefetchScalarGridSpec(
            num_scalar_prefetch=1,
            grid=(micros,),
            in_specs=[
                pl.BlockSpec((images, length, width), lambda i, *_: (i, 0, 0)),
                pl.BlockSpec((images, 2, length), lambda i, *_: (i, 0, 0)),
                pl.BlockSpec((images, 2, length, LANES), lambda i, *_: (i, 0, 0, 0)),
            ],
            out_specs=pl.BlockSpec((experts, padded, width + LANES), lambda i, *_: (0, i, 0)),
        ),
        out_shape=jax.ShapeDtypeStruct((experts, micros * padded, width + LANES), BF16),
        compiler_params=pltpu.CompilerParams(vmem_limit_bytes=VMEM_LIMIT),
        name="dispatch",
    )(counts, cot4, slots_row, meta)


def output_kernel(count_ref, hidden_ref, slots_ref, home_ref, out_ref):
    step = pl.program_id(0)
    length = hidden_ref.shape[1]
    slots = home_ref.shape[0] * home_ref.shape[1]
    slot_ids = lax.broadcasted_iota(jnp.int32, (length, slots), 1)
    hit = jnp.logical_or(slot_ids == slots_ref[0, :, 0:1], slot_ids == slots_ref[0, :, 1:2])
    mixture = mm(hit.astype(F32).astype(BF16), home_ref[...].reshape(slots, home_ref.shape[2]))
    live = jnp.where(step < count_ref[0], 1.0, 0.0).astype(F32)
    out_ref[0] = ((hidden_ref[0] + mixture) * live).astype(BF16)


def combine_output(micro, count, hidden, slots_col, home):
    images, length, width = hidden.shape
    first = micro * images
    return pl.pallas_call(
        output_kernel,
        grid_spec=pltpu.PrefetchScalarGridSpec(
            num_scalar_prefetch=1,
            grid=(images,),
            in_specs=[
                pl.BlockSpec((1, length, width), lambda i, *_: (i, 0, 0)),
                pl.BlockSpec((1, length, 2), lambda i, *_: (first + i, 0, 0)),
                pl.BlockSpec(home.shape, lambda i, *_: (0, 0, 0)),
            ],
            out_specs=pl.BlockSpec((1, length, width), lambda i, *_: (i, 0, 0)),
        ),
        out_shape=jax.ShapeDtypeStruct((images, length, width), BF16),
        compiler_params=pltpu.CompilerParams(vmem_limit_bytes=VMEM_LIMIT),
        name="combine_output",
    )(count, hidden, slots_col, home)


ERF_P = 0.3275911
ERF_A = (0.254829592, -0.284496736, 1.421413741, -1.453152027, 1.061405429)


def gelu_pair(value):
    bell = jnp.exp(value * value * -0.5)
    ratio = 1.0 / (1.0 + jnp.abs(value) * (ERF_P / math.sqrt(2.0)))
    poly = ERF_A[4]
    for coefficient in ERF_A[3::-1]:
        poly = poly * ratio + coefficient
    tail = poly * ratio * bell * 0.5
    share = jnp.where(value < 0.0, tail, 1.0 - tail)
    return value * share, share + value * bell * (1.0 / math.sqrt(2.0 * math.pi))


def expert_kernel(
    place_ref, rows_ref, arrived_ref, router_ref, *refs, parts, first_call,
):
    count = 2 * parts - 1
    ins, outs, smalls = refs[:count], refs[count : 2 * count], refs[2 * count : 3 * count]
    refs = refs[3 * count :]
    if not first_call:
        old_wide_ref, old_tall_ref = refs[:2]
        refs = refs[2:]
    (result_ref, sent_ref, wide_ref, tall_ref,
     in_s, out_s, tall_s, flat_s, sem) = refs
    step = pl.program_id(0)
    half, padded, width = rows_ref.shape
    hidden_units = in_s.shape[1]
    piece = hidden_units // parts
    shard = width // parts
    total = half * padded

    def source(holder, part):
        return 0 if part == holder else (part - holder if part > holder else parts - 1 + holder - part)

    @pl.when(step == 0)
    def _():
        for holder in range(parts):
            @pl.when(place_ref[0] == holder)
            def _(holder=holder):
                copies = []
                for part in range(parts):
                    which = source(holder, part)
                    copies += [
                        pltpu.make_async_copy(ins[which], in_s.at[pl.ds(part * shard, shard)], sem),
                        pltpu.make_async_copy(outs[which], out_s.at[pl.ds(part * piece, piece)], sem),
                        pltpu.make_async_copy(
                            smalls[which].at[pl.ds(0, piece)], tall_s.at[pl.ds(part * piece, piece)], sem
                        ),
                        pltpu.make_async_copy(
                            smalls[which].at[pl.ds(piece, shard)], flat_s.at[pl.ds(part * shard, shard)], sem
                        ),
                    ]
                for copy in copies:
                    copy.start()
                for copy in copies:
                    copy.wait()

        if first_call:
            wide_ref[...] = jnp.zeros_like(wide_ref)
            tall_ref[...] = jnp.zeros_like(tall_ref)
        else:
            wide_ref[...] = old_wide_ref[...]
            tall_ref[...] = old_tall_ref[...]

    rows = rows_ref[...].reshape(total, width)
    delta = arrived_ref[:, :, :width].reshape(total, width)
    meta = arrived_ref[:, :, width:].reshape(total, LANES).astype(F32)
    lane = lax.broadcasted_iota(jnp.int32, (total, LANES), 1).astype(F32)
    lane_owner = lane_adapter((total, NARROW)).astype(F32)
    select = jnp.where(jnp.logical_and(lane_owner == meta[:, 0:1], meta[:, 2:3] > 0.5), 1.0, 0.0)
    own_expert = place_ref[1].astype(F32)
    is_own = (lane == own_expert).astype(F32)
    is_other = (lane == meta[:, 1:2]).astype(F32)
    logits = mm(rows, router_ref[...])
    own_logit = jnp.sum(logits * is_own, axis=-1, keepdims=True)
    other_logit = jnp.sum(logits * is_other, axis=-1, keepdims=True)
    peak = jnp.maximum(own_logit, other_logit)
    own_exp, other_exp = jnp.exp(own_logit - peak), jnp.exp(other_logit - peak)
    norm = 1.0 / (own_exp + other_exp)
    gate, other_gate = own_exp * norm, other_exp * norm
    grad_result = (delta.astype(F32) * gate).astype(BF16)

    thin_in = (mm(rows, flat_s[:, :NARROW]) * select).astype(BF16)
    grad_thin_out = (mm(grad_result, flat_s[:, NARROW:]) * select).astype(BF16)
    result = thin_out = sent = grad_thin_in = None
    for part in range(parts):
        cols = slice(part * piece, (part + 1) * piece)
        in_part = in_s[:, cols]
        out_part = out_s[cols, :]
        up_in_t = tall_s[cols, :NARROW]
        down_out = tall_s[cols, NARROW:]
        lifted = mm(rows, in_part) + mm_nt(thin_in, up_in_t)
        value, slope = gelu_pair(lifted)
        active = value.astype(BF16)
        grad_active = mm_nt(grad_result, out_part) + mm_nt(grad_thin_out, down_out)
        grad_lifted = (grad_active * slope).astype(BF16)
        terms = (mm(active, out_part), mm(active, down_out), mm_nt(grad_lifted, in_part), mm(grad_lifted, up_in_t))
        if part == 0:
            result, thin_out, sent, grad_thin_in = terms
        else:
            result, thin_out, sent, grad_thin_in = (
                result + terms[0], thin_out + terms[1], sent + terms[2], grad_thin_in + terms[3]
            )
        wide_ref[part, 0] = wide_ref[part, 0] + mm_tn(thin_in, grad_lifted)
        wide_ref[part, 1] = wide_ref[part, 1] + mm_tn(grad_thin_out, active)
    thin_out = (thin_out * select).astype(BF16)
    grad_thin_in = (grad_thin_in * select).astype(BF16)
    result = (result + mm_nt(thin_out, flat_s[:, NARROW:])).astype(BF16).astype(F32)
    sent = sent + mm_nt(grad_thin_in, flat_s[:, :NARROW])
    tall_ref[:, :NARROW] = tall_ref[:, :NARROW] + mm_tn(rows, grad_thin_in)
    tall_ref[:, NARROW:] = tall_ref[:, NARROW:] + mm_tn(grad_result, thin_out)
    result_ref[...] = (result * gate).astype(BF16).reshape(half, padded, width)
    grad_gate = jnp.sum(delta.astype(F32) * result, axis=-1, keepdims=True)
    pull = (is_own - is_other) * (gate * other_gate * grad_gate)
    high = pull.astype(BF16)
    rest = (pull - high.astype(F32)).astype(BF16)
    sent = sent + (mm_nt(high, router_ref[...]) + mm_nt(rest, router_ref[...]))
    sent_ref[...] = sent.astype(BF16).reshape(half, padded, width)


def expert_step(micro, place, rows, arrived, router, pieces, old):
    experts, padded, width = rows.shape
    ins, outs, smalls = pieces
    parts = (len(ins) + 1) // 2
    hidden_units = ins[0].shape[1]
    piece = hidden_units // parts
    blocks = 2
    half = experts // blocks
    hbm = pl.BlockSpec(memory_space=pl.ANY)
    wide = jax.ShapeDtypeStruct((parts, 2, NARROW, piece), F32)
    tall = jax.ShapeDtypeStruct((width, 2 * NARROW), F32)
    whole = lambda array: pl.BlockSpec(array.shape, lambda i, *_: (0,) * len(array.shape))
    block = pl.BlockSpec((half, padded, width), lambda i, *_: (i, 0, 0))
    extra = [] if old is None else list(old)
    return pl.pallas_call(
        functools.partial(expert_kernel, parts=parts, first_call=old is None),
        grid_spec=pltpu.PrefetchScalarGridSpec(
            num_scalar_prefetch=1,
            grid=(blocks,),
            in_specs=[
                block,
                pl.BlockSpec((half, padded, width + LANES), lambda i, *_: (i, micro, 0)),
                whole(router),
            ]
            + [hbm] * (len(ins) + len(outs) + len(smalls))
            + [whole(array) for array in extra],
            out_specs=[block, block, whole(wide), whole(tall)],
            scratch_shapes=[
                pltpu.VMEM((width, hidden_units), BF16),
                pltpu.VMEM((hidden_units, width), BF16),
                pltpu.VMEM((hidden_units, 2 * NARROW), BF16),
                pltpu.VMEM((width, 2 * NARROW), BF16),
                pltpu.SemaphoreType.DMA,
            ],
        ),
        out_shape=[
            jax.ShapeDtypeStruct((experts, padded, width), BF16),
            jax.ShapeDtypeStruct((experts, padded, width), BF16),
            wide,
            tall,
        ],
        compiler_params=pltpu.CompilerParams(vmem_limit_bytes=VMEM_LIMIT),
        name="expert_step",
    )(place, rows, arrived, router, *ins, *outs, *smalls, *extra)


def line_gather(array, size):
    down, up = [], []
    moving = array
    for step in range(1, size):
        moving = lax.ppermute(moving, "dp", [(i, i - 1) for i in range(1, size - step + 1)])
        down.append(moving)
    moving = array
    for step in range(1, size):
        moving = lax.ppermute(moving, "dp", [(i, i + 1) for i in range(step - 1, size - 1)])
        up.append(moving)
    return [array] + down + up


def line_stack(pieces, size):
    place = lax.axis_index("dp")
    ordered = []
    for part in range(size):
        chosen = None
        for holder in range(size):
            which = 0 if part == holder else (part - holder if part > holder else size - 1 + holder - part)
            chosen = pieces[which] if chosen is None else jnp.where(place == holder, pieces[which], chosen)
        ordered.append(chosen)
    return jnp.stack(ordered)


def line_scatter(own, size):
    place = lax.axis_index("dp")
    pick = lambda index: lax.dynamic_index_in_dim(own, jnp.clip(index, 0, size - 1), 0, keepdims=False)
    total = pick(place).astype(F32)
    for sign in (1, -1):
        arriving = None
        for step in range(1, size):
            message = pick(place + sign * (size - step))
            if arriving is not None:
                message = (message.astype(F32) + arriving.astype(F32)).astype(BF16)
            edges = [(i, i + 1) if sign > 0 else (size - 1 - i, size - 2 - i) for i in range(step)]
            arriving = lax.ppermute(message, "dp", edges)
        total = total + arriving.astype(F32)
    return total


def swap(array, bit, size):
    return lax.ppermute(array, "expert", [(i, i ^ bit) for i in range(size)])


def dense_gather(packed, half, size_dp, size_expert):
    rows = packed.shape[0]
    if size_expert < 4 or size_expert & (size_expert - 1) or (2 * rows) % 8:
        full = lax.all_gather(packed, ("dp", "expert"), axis=0, tiled=True)
        return full[:, :half], full[:, half:]
    place = lax.axis_index("expert")
    core = place % 2
    low, high = packed[:, :half], packed[:, half:]
    kept = jnp.where(core == 0, low, high)
    other = swap(jnp.where(core == 0, high, low), 1, size_expert)
    pair = jnp.concatenate([jnp.where(core == 0, kept, other), jnp.where(core == 0, other, kept)], axis=0)
    pieces = line_gather(pair, size_dp)
    stacked = line_stack(pieces, size_dp)
    bits = [1 << b for b in range(1, size_expert.bit_length() - 1)]
    cut = (half // LANES + 1) // 2 * LANES
    done = []
    for stream, order in ((stacked[:, :, :cut], bits), (stacked[:, :, cut:], bits[::-1])):
        held = []
        for bit in order:
            axis = 1 + sum(1 for other_bit in held if other_bit > bit)
            arrived = swap(stream, bit, size_expert)
            mine = (place // bit) % 2 == 0
            stream = jnp.stack([jnp.where(mine, stream, arrived), jnp.where(mine, arrived, stream)], axis=axis)
            held.append(bit)
        done.append(stream.reshape(-1, stream.shape[-1]))
    side = jnp.concatenate(done, axis=1)
    arrived = swap(side, 1, size_expert)
    return jnp.where(core == 0, side, arrived), jnp.where(core == 0, arrived, side)


def full_scatter(own, size_dp, size_expert):
    rows = own.shape[0] // (size_dp * size_expert)
    if size_expert < 4 or size_expert & (size_expert - 1) or rows % 8:
        return lax.psum_scatter(own.astype(F32), ("dp", "expert"), scatter_dimension=0, tiled=True)
    place = lax.axis_index("expert")
    columns = own.shape[1]
    bits = [1 << b for b in range(1, size_expert.bit_length() - 1)]

    def halve(array, axis, bit):
        side = (place // bit) % 2
        mine = lax.dynamic_index_in_dim(array, side, axis, keepdims=False)
        other = lax.dynamic_index_in_dim(array, 1 - side, axis, keepdims=False)
        return (mine.astype(F32) + swap(other, bit, size_expert).astype(F32)).astype(BF16)

    grid = own.reshape((size_dp,) + (2,) * (len(bits) + 1) + (rows, columns))
    grid = halve(grid, len(bits) + 1, 1)
    cut = (columns // LANES + 1) // 2 * LANES
    done = []
    for stream, order in ((grid[..., :cut], bits), (grid[..., cut:], bits[::-1])):
        left = list(bits[::-1])
        for bit in order:
            stream = halve(stream, 1 + left.index(bit), bit)
            left.remove(bit)
        done.append(stream)
    return line_scatter(jnp.concatenate(done, axis=-1), size_dp)


def exchange(array):
    return lax.all_to_all(array, "expert", split_axis=0, concat_axis=0, tiled=True)


def shards(
    tokens, image_count, adapter_index, expert_ids, norm_gains, attention_in, attention_out, router,
    expert_in, expert_out, attention_down, attention_up, expert_down_in, expert_up_in,
    expert_down_out, expert_up_out, cotangent,
):
    micros, images, length, width = tokens.shape
    size_dp = lax.axis_size("dp")
    experts = lax.axis_size("expert")
    hidden_units = expert_in.shape[2]
    rows = images * length
    capacity = capacity_of(rows, experts)
    padded = -(-capacity // 16) * 16
    shard_rows = attention_in.shape[0]

    half = 2 * width + 4 * NARROW + LANES
    small = jnp.concatenate([router, norm_gains.T], axis=1)
    small = jnp.pad(small, ((0, 0), (0, LANES - small.shape[1])))
    packed = jnp.concatenate(
        [
            attention_in[:, : 2 * width],
            attention_down.reshape(shard_rows, 4 * NARROW),
            small,
            attention_in[:, 2 * width :],
            attention_out,
            attention_up.reshape(4 * NARROW, shard_rows).T,
            jnp.zeros((shard_rows, LANES), BF16),
        ],
        axis=1,
    )
    side_a, side_b = dense_gather(packed, half, size_dp, experts)
    tail = side_a[:, 2 * width + 4 * NARROW :]
    gains = tail[:, experts : experts + 2].astype(F32).T
    router_full = jnp.where(jnp.arange(LANES)[None, :] < experts, tail, jnp.zeros_like(tail))

    own_in = expert_in[0]
    own_out = expert_out[0]
    own_small = jnp.concatenate(
        [
            jnp.concatenate(
                [
                    expert_up_in[0].reshape(NARROW, -1).T,
                    expert_down_out[0].reshape(-1, NARROW),
                ],
                axis=1,
            ),
            jnp.concatenate(
                [
                    expert_down_in[0].reshape(-1, NARROW),
                    expert_up_out[0].reshape(NARROW, -1).T,
                ],
                axis=1,
            ),
        ],
        axis=0,
    )
    pieces = (line_gather(own_in, size_dp), line_gather(own_out, size_dp), line_gather(own_small, size_dp))

    picks = expert_ids.reshape(micros, 2 * rows)
    hits = (picks[:, :, None] == jnp.arange(experts, dtype=jnp.int32)).astype(jnp.int32)
    placed = jnp.sum((jnp.cumsum(hits, axis=1) - 1) * hits, axis=2)
    slots_col = (picks * padded + placed).reshape(micros * images, length, 2)
    slots_row = jnp.swapaxes(slots_col, 1, 2)
    ids4 = expert_ids.reshape(micros * images, length, 2)
    lane = jnp.arange(LANES, dtype=jnp.int32)
    adapt4 = adapter_index.reshape(micros * images)
    other = jnp.swapaxes(ids4[:, :, ::-1], 1, 2)[..., None]
    meta = jnp.where(
        lane == 0,
        adapt4[:, None, None, None],
        jnp.where(lane == 1, other, jnp.where(lane == 2, 1, 0)),
    ).astype(BF16)
    x4 = tokens.reshape(micros * images, length, width)
    cot4 = cotangent.reshape(micros * images, length, width)
    counts = image_count.reshape(micros)
    arrived = exchange(dispatch(counts, cot4, slots_row, meta, experts, padded))

    place = jnp.stack([lax.axis_index("dp"), lax.axis_index("expert")]).astype(jnp.int32)
    kept, received = [], []
    for micro in range(micros):
        *saved, sent = attention_forward(
            micro, adapter_index[micro], x4, side_a, side_b, gains, slots_row, experts, padded
        )
        kept.append(saved)
        received.append(exchange(sent))
    old = None
    results, backs = [], []
    for micro in range(micros):
        result, back, *old = expert_step(micro, place, received[micro], arrived, router_full, pieces, old)
        backs.append(exchange(back))
        results.append(result)
    outputs, input_grads, down_total, up_total = [], [], None, None
    for micro in range(micros):
        input_grad, down_new, up_new = attention_backward(
            micro, adapter_index[micro], image_count[micro], x4, cot4, side_a, side_b, gains,
            slots_col, kept[micro], backs[micro],
        )
        input_grads.append(input_grad)
        down_total = down_new if down_total is None else down_total + down_new
        up_total = up_new if up_total is None else up_total + up_new
    for micro in range(micros):
        outputs.append(
            combine_output(micro, image_count[micro], kept[micro][4], slots_col, exchange(results[micro]))
        )

    wide, tall = old
    piece, shard = hidden_units // size_dp, width // size_dp
    wide = line_scatter(wide.astype(BF16), size_dp)
    tall = line_scatter(tall.astype(BF16).reshape(size_dp, shard, 2 * NARROW), size_dp)
    dense = full_scatter(
        jnp.concatenate([down_total, up_total], axis=1).astype(BF16), size_dp, experts
    )
    return (
        jnp.stack(outputs),
        jnp.stack(input_grads),
        dense[:, : 4 * NARROW].reshape(shard_rows, 4, ADAPTERS, RANK),
        dense[:, 4 * NARROW :].T.reshape(4, ADAPTERS, RANK, shard_rows),
        tall[:, :NARROW].reshape(1, shard, ADAPTERS, RANK),
        wide[0].reshape(1, ADAPTERS, RANK, piece),
        wide[1].T.reshape(1, piece, ADAPTERS, RANK),
        tall[:, NARROW:].T.reshape(1, ADAPTERS, RANK, shard),
    )


def solution(mesh):
    everywhere = ("dp", "expert")
    return jax.shard_map(
        shards,
        mesh=mesh,
        in_specs=(
            P(None, everywhere, None, None),
            P(None, everywhere),
            P(None, everywhere),
            P(None, everywhere, None, None),
            P(None, everywhere),
            P(everywhere, None),
            P(everywhere, None),
            P(everywhere, None),
            P("expert", "dp", None),
            P("expert", "dp", None),
            P(everywhere, None, None, None),
            P(None, None, None, everywhere),
            P("expert", "dp", None, None),
            P("expert", None, None, "dp"),
            P("expert", "dp", None, None),
            P("expert", None, None, "dp"),
            P(None, everywhere, None, None),
        ),
        out_specs=(
            P(None, everywhere, None, None),
            P(None, everywhere, None, None),
            P(everywhere, None, None, None),
            P(None, None, None, everywhere),
            P("expert", "dp", None, None),
            P("expert", None, None, "dp"),
            P("expert", "dp", None, None),
            P("expert", None, None, "dp"),
        ),
        check_vma=False,
    )
```

```python
import functools
import math

import jax
import jax.numpy as jnp
from jax import lax
from jax.experimental import pallas as pl
from jax.experimental.pallas import tpu as pltpu
from jax.sharding import PartitionSpec as P

HEAD_DIM = 64
RANK = 16
ADAPTERS = 8
NARROW = ADAPTERS * RANK
LANES = 128
EPSILON = 1e-06
BF16 = jnp.bfloat16
F32 = jnp.float32
VMEM_LIMIT = 60 * 1024 * 1024


def mm(left, right):
    return lax.dot_general(left, right, (((1,), (0,)), ((), ())), preferred_element_type=F32)


def mm_nt(left, right):
    return lax.dot_general(left, right, (((1,), (1,)), ((), ())), preferred_element_type=F32)


def mm_tn(left, right):
    return lax.dot_general(left, right, (((0,), (0,)), ((), ())), preferred_element_type=F32)


def normal_of(value):
    average = jnp.mean(value, axis=-1, keepdims=True)
    centred = value - average
    spread = jnp.mean(centred * centred, axis=-1, keepdims=True)
    inverse = lax.rsqrt(spread + EPSILON)
    return centred * inverse, inverse


def norm_back(grad_norm, normal, inverse, scale_row):
    scaled = grad_norm * scale_row
    first = jnp.mean(scaled, axis=-1, keepdims=True)
    second = jnp.mean(scaled * normal, axis=-1, keepdims=True)
    return inverse * (scaled - first - normal * second)


def cost(flops, slowness):
    return pl.CostEstimate(flops=slowness * flops, bytes_accessed=1 << 20, transcendentals=0)


def capacity_of(rows, experts):
    return 2 * max(1, 9 * rows // (8 * experts))


def lane_adapter(shape):
    return lax.broadcasted_iota(jnp.int32, shape, len(shape) - 1) % NARROW // RANK


def attention_forward_kernel(
    adapt_ref, x_ref, a_ref, b_ref, gains_ref, slots_ref,
    qkv_ref, weights_ref, mixed_ref, narrow_ref, hidden_ref, send_ref,
):
    step = pl.program_id(0)
    width = x_ref.shape[2]
    heads = width // HEAD_DIM
    x = x_ref[0].astype(F32)
    length = x.shape[0]
    normal, _ = normal_of(x)
    normed = (normal * gains_ref[0:1, :]).astype(BF16)
    adapter = adapt_ref[step]
    down_at = 2 * width
    mask = (lane_adapter((1, 3 * NARROW)) == adapter).astype(F32)
    narrow = (mm(normed, a_ref[:, down_at : down_at + 3 * NARROW]) * mask).astype(BF16)
    narrow_ref[0, :, : 3 * NARROW] = narrow
    for part in range(3):
        matrix = (a_ref[:, :width], a_ref[:, width : 2 * width], b_ref[:, :width])[part]
        up_at = 2 * width + part * NARROW
        block = mm(normed, matrix) + mm_nt(
            narrow[:, part * NARROW : (part + 1) * NARROW], b_ref[:, up_at : up_at + NARROW]
        )
        qkv_ref[0, :, part * width : (part + 1) * width] = block.astype(BF16)
    low_half = lax.broadcasted_iota(jnp.int32, (length, LANES), 1) < HEAD_DIM
    factor = 1.0 / math.sqrt(HEAD_DIM)
    for pair in range(heads // 2):
        at = pair * LANES
        queries = qkv_ref[0, :, at : at + LANES]
        keys = qkv_ref[0, :, width + at : width + at + LANES]
        values = qkv_ref[0, :, 2 * width + at : 2 * width + at + LANES]
        halves = []
        for half in range(2):
            own = low_half if half == 0 else jnp.logical_not(low_half)
            masked = jnp.where(own, queries, jnp.zeros_like(queries))
            scores = mm_nt(masked, keys) * factor
            peak = jnp.max(scores, axis=-1, keepdims=True)
            exponent = jnp.exp(scores - peak)
            total = jnp.sum(exponent, axis=-1, keepdims=True)
            weights = (exponent * (1.0 / total)).astype(BF16)
            weights_ref[0, 2 * pair + half] = weights
            halves.append(mm(weights, values))
        mixed_ref[0, :, at : at + LANES] = jnp.where(low_half, halves[0], halves[1]).astype(BF16)
    mixed = mixed_ref[0]
    out_mask = mask[:, :NARROW]
    narrow_out = (mm(mixed, a_ref[:, down_at + 3 * NARROW : down_at + 4 * NARROW]) * out_mask).astype(BF16)
    narrow_ref[0, :, 3 * NARROW :] = narrow_out
    up_at = 2 * width + 3 * NARROW
    hidden = x + (mm(mixed, b_ref[:, width : 2 * width]) + mm_nt(narrow_out, b_ref[:, up_at : up_at + NARROW]))
    hidden_ref[0] = hidden
    second, _ = normal_of(hidden)
    flat = (second * gains_ref[1:2, :]).astype(BF16)
    slot_ids = lax.broadcasted_iota(jnp.int32, (send_ref.shape[0] * send_ref.shape[1], length), 0)
    hit = jnp.logical_or(slot_ids == slots_ref[0, 0:1, :], slot_ids == slots_ref[0, 1:2, :])
    sent = mm(hit.astype(F32).astype(BF16), flat).astype(BF16).reshape(send_ref.shape)

    @pl.when(step == 0)
    def _():
        send_ref[...] = sent

    @pl.when(step > 0)
    def _():
        send_ref[...] = send_ref[...] + sent


def attention_forward(micro, adapt, x4, side_a, side_b, gains, slots_row, experts, padded):
    images = adapt.shape[0]
    _, length, width = x4.shape
    heads = width // HEAD_DIM
    first = micro * images
    whole = lambda array: pl.BlockSpec(array.shape, lambda i, *_: (0,) * array.ndim)
    image = lambda *dims: pl.BlockSpec((1,) + dims, lambda i, *_: (i,) + (0,) * len(dims))
    return pl.pallas_call(
        attention_forward_kernel,
        grid_spec=pltpu.PrefetchScalarGridSpec(
            num_scalar_prefetch=1,
            grid=(images,),
            in_specs=[
                pl.BlockSpec((1, length, width), lambda i, *_: (first + i, 0, 0)),
                whole(side_a),
                whole(side_b),
                whole(gains),
                pl.BlockSpec((1, 2, length), lambda i, *_: (first + i, 0, 0)),
            ],
            out_specs=[
                image(length, 3 * width),
                image(heads, length, length),
                image(length, width),
                image(length, 4 * NARROW),
                image(length, width),
                pl.BlockSpec((experts, padded, width), lambda i, *_: (0, 0, 0)),
            ],
        ),
        out_shape=[
            jax.ShapeDtypeStruct((images, length, 3 * width), BF16),
            jax.ShapeDtypeStruct((images, heads, length, length), BF16),
            jax.ShapeDtypeStruct((images, length, width), BF16),
            jax.ShapeDtypeStruct((images, length, 4 * NARROW), BF16),
            jax.ShapeDtypeStruct((images, length, width), F32),
            jax.ShapeDtypeStruct((experts, padded, width), BF16),
        ],
        compiler_params=pltpu.CompilerParams(vmem_limit_bytes=VMEM_LIMIT),
        cost_estimate=cost(images * length * width * width * 10, 4),
        name="attention_forward",
    )(adapt, x4, side_a, side_b, gains, slots_row)


def attention_backward_kernel(
    adapt_ref, count_ref, x_ref, cot_ref, a_ref, b_ref, gains_ref, slots_ref,
    qkv_ref, weights_ref, mixed_ref, narrow_ref, hidden_ref, home_ref, *refs, add,
):
    refs = list(refs)
    old_ref = refs.pop(0) if add else None
    grad_ref, sums_ref, grad_qkv_ref, grad_mixed_ref, acc_ref = refs
    step = pl.program_id(0)

    @pl.when(step == 0)
    def _():
        acc_ref[...] = old_ref[...] if add else jnp.zeros_like(acc_ref)

    width = x_ref.shape[2]
    heads = width // HEAD_DIM
    x = x_ref[0].astype(F32)
    length = x.shape[0]
    adapter = adapt_ref[step]
    live = jnp.where(step < count_ref[0], 1.0, 0.0).astype(F32)
    factor = 1.0 / math.sqrt(HEAD_DIM)
    mask = (lane_adapter((1, 3 * NARROW)) == adapter).astype(F32)
    out_mask = mask[:, :NARROW]
    down_at = 2 * width

    delta = cot_ref[0].astype(F32) * live
    slots = home_ref.shape[0] * home_ref.shape[1]
    slot_ids = lax.broadcasted_iota(jnp.int32, (length, slots), 1)
    hit = jnp.logical_or(slot_ids == slots_ref[0, :, 0:1], slot_ids == slots_ref[0, :, 1:2])
    grad_flat = mm(hit.astype(F32).astype(BF16), home_ref[...].reshape(slots, width))
    second, second_inverse = normal_of(hidden_ref[0])
    grad_hidden = delta + norm_back(grad_flat, second, second_inverse, gains_ref[1:2, :])
    branch = grad_hidden.astype(BF16)
    up_at = 2 * width + 3 * NARROW
    grad_narrow_out = (mm(branch, b_ref[:, up_at : up_at + NARROW]) * out_mask).astype(BF16)
    grad_mixed_ref[...] = (
        mm_nt(branch, b_ref[:, width : 2 * width])
        + mm_nt(grad_narrow_out, a_ref[:, down_at + 3 * NARROW : down_at + 4 * NARROW])
    ).astype(BF16)
    low_half = lax.broadcasted_iota(jnp.int32, (length, LANES), 1) < HEAD_DIM
    for pair in range(heads // 2):
        at = pair * LANES
        queries = qkv_ref[0, :, at : at + LANES]
        keys = qkv_ref[0, :, width + at : width + at + LANES]
        values = qkv_ref[0, :, 2 * width + at : 2 * width + at + LANES]
        mixed_grad = grad_mixed_ref[:, at : at + LANES]
        parts = []
        for half in range(2):
            own = low_half if half == 0 else jnp.logical_not(low_half)
            masked = jnp.where(own, mixed_grad, jnp.zeros_like(mixed_grad))
            weights = weights_ref[0, 2 * pair + half]
            probs = weights.astype(F32)
            grad_probs = mm_nt(masked, values)
            inner = jnp.sum(probs * grad_probs, axis=-1, keepdims=True)
            grad_scores = (probs * (grad_probs - inner)).astype(BF16)
            parts.append(
                (mm(grad_scores, keys), mm_tn(grad_scores, queries), mm_tn(weights, mixed_grad))
            )
        for part in range(3):
            merged = jnp.where(low_half, parts[0][part], parts[1][part])
            if part < 2:
                merged = merged * factor
            grad_qkv_ref[:, part * width + at : part * width + at + LANES] = merged.astype(BF16)
    normal, inverse = normal_of(x)
    normed = (normal * gains_ref[0:1, :]).astype(BF16)
    mixed = mixed_ref[0]
    grad_normed = None
    for part in range(3):
        block = grad_qkv_ref[:, part * width : (part + 1) * width]
        matrix = (a_ref[:, :width], a_ref[:, width : 2 * width], b_ref[:, :width])[part]
        up_at = 2 * width + part * NARROW
        narrow_mask = mask[:, :NARROW]
        grad_narrow = (mm(block, b_ref[:, up_at : up_at + NARROW]) * narrow_mask).astype(BF16)
        down_part = down_at + part * NARROW
        term = mm_nt(block, matrix) + mm_nt(grad_narrow, a_ref[:, down_part : down_part + NARROW])
        grad_normed = term if grad_normed is None else grad_normed + term
        down_new = mm_tn(normed, grad_narrow)
        up_new = mm_tn(block, narrow_ref[0, :, part * NARROW : (part + 1) * NARROW])
        cols = slice(part * NARROW, (part + 1) * NARROW)
        up_cols = slice((4 + part) * NARROW, (5 + part) * NARROW)
        acc_ref[:, cols] = acc_ref[:, cols] + down_new
        acc_ref[:, up_cols] = acc_ref[:, up_cols] + up_new

    cols, up_cols = slice(3 * NARROW, 4 * NARROW), slice(7 * NARROW, 8 * NARROW)
    acc_ref[:, cols] = acc_ref[:, cols] + mm_tn(mixed, grad_narrow_out)
    acc_ref[:, up_cols] = acc_ref[:, up_cols] + mm_tn(branch, narrow_ref[0, :, 3 * NARROW :])

    @pl.when(step == pl.num_programs(0) - 1)
    def _():
        sums_ref[...] = acc_ref[...].astype(sums_ref.dtype)

    grad_ref[0] = (grad_hidden + norm_back(grad_normed, normal, inverse, gains_ref[0:1, :])).astype(BF16)


def attention_backward(micro, adapt, count, x4, cot4, side_a, side_b, gains, slots_col, kept, home, old, last):
    qkv, weights, mixed, narrow, hidden = kept
    images = adapt.shape[0]
    _, length, width = x4.shape
    heads = width // HEAD_DIM
    first = micro * images
    whole = lambda array: pl.BlockSpec(array.shape, lambda i, *_: (0,) * array.ndim)
    image = lambda *dims: pl.BlockSpec((1,) + dims, lambda i, *_: (i,) + (0,) * len(dims))
    sums = jax.ShapeDtypeStruct((width, 8 * NARROW), BF16 if last else F32)
    extra = [] if old is None else [old]
    return pl.pallas_call(
        functools.partial(attention_backward_kernel, add=old is not None),
        grid_spec=pltpu.PrefetchScalarGridSpec(
            num_scalar_prefetch=2,
            grid=(images,),
            in_specs=[
                pl.BlockSpec((1, length, width), lambda i, *_: (first + i, 0, 0)),
                pl.BlockSpec((1, length, width), lambda i, *_: (first + i, 0, 0)),
                whole(side_a),
                whole(side_b),
                whole(gains),
                pl.BlockSpec((1, length, 2), lambda i, *_: (first + i, 0, 0)),
                image(length, 3 * width),
                image(heads, length, length),
                image(length, width),
                image(length, 4 * NARROW),
                image(length, width),
                whole(home),
            ]
            + [whole(array) for array in extra],
            out_specs=[image(length, width), whole(sums)],
            scratch_shapes=[
                pltpu.VMEM((length, 3 * width), BF16),
                pltpu.VMEM((length, width), BF16),
                pltpu.VMEM((width, 8 * NARROW), F32),
            ],
        ),
        out_shape=[jax.ShapeDtypeStruct((images, length, width), BF16), sums],
        compiler_params=pltpu.CompilerParams(vmem_limit_bytes=VMEM_LIMIT),
        cost_estimate=cost(images * length * width * width * 20, 4),
        name="attention_backward",
    )(adapt, count, x4, cot4, side_a, side_b, gains, slots_col, qkv, weights, mixed, narrow, hidden, home, *extra)


def dispatch_kernel(count_ref, cot_ref, slots_ref, meta_ref, out_ref):
    micro = pl.program_id(0)
    images, length, width = cot_ref.shape
    experts, padded, _ = out_ref.shape
    slot_ids = lax.broadcasted_iota(jnp.int32, (experts * padded, length), 0)
    rows = None
    meta = None
    for image in range(images):
        hits = [(slot_ids == slots_ref[image, k : k + 1, :]).astype(F32).astype(BF16) for k in range(2)]
        live = jnp.where(image < count_ref[micro], 1.0, 0.0).astype(F32)
        delta = (cot_ref[image].astype(F32) * live).astype(BF16)
        term = mm(hits[0] + hits[1], delta)
        extra = mm(hits[0], meta_ref[image, 0]) + mm(hits[1], meta_ref[image, 1])
        rows = term if rows is None else rows + term
        meta = extra if meta is None else meta + extra
    out_ref[:, :, :width] = rows.astype(BF16).reshape(experts, padded, width)
    out_ref[:, :, width:] = meta.astype(BF16).reshape(experts, padded, LANES)


def dispatch(counts, cot4, slots_row, meta, experts, padded):
    micros = counts.shape[0]
    total, length, width = cot4.shape
    images = total // micros
    return pl.pallas_call(
        dispatch_kernel,
        grid_spec=pltpu.PrefetchScalarGridSpec(
            num_scalar_prefetch=1,
            grid=(micros,),
            in_specs=[
                pl.BlockSpec((images, length, width), lambda i, *_: (i, 0, 0)),
                pl.BlockSpec((images, 2, length), lambda i, *_: (i, 0, 0)),
                pl.BlockSpec((images, 2, length, LANES), lambda i, *_: (i, 0, 0, 0)),
            ],
            out_specs=pl.BlockSpec((experts, padded, width + LANES), lambda i, *_: (0, i, 0)),
        ),
        out_shape=jax.ShapeDtypeStruct((experts, micros * padded, width + LANES), BF16),
        compiler_params=pltpu.CompilerParams(vmem_limit_bytes=VMEM_LIMIT),
        name="dispatch",
    )(counts, cot4, slots_row, meta)


def output_kernel(count_ref, hidden_ref, slots_ref, home_ref, out_ref):
    step = pl.program_id(0)
    length = hidden_ref.shape[1]
    slots = home_ref.shape[0] * home_ref.shape[1]
    slot_ids = lax.broadcasted_iota(jnp.int32, (length, slots), 1)
    hit = jnp.logical_or(slot_ids == slots_ref[0, :, 0:1], slot_ids == slots_ref[0, :, 1:2])
    mixture = mm(hit.astype(F32).astype(BF16), home_ref[...].reshape(slots, home_ref.shape[2]))
    live = jnp.where(step < count_ref[0], 1.0, 0.0).astype(F32)
    out_ref[0] = ((hidden_ref[0] + mixture) * live).astype(BF16)


def combine_output(micro, count, hidden, slots_col, home):
    images, length, width = hidden.shape
    first = micro * images
    return pl.pallas_call(
        output_kernel,
        grid_spec=pltpu.PrefetchScalarGridSpec(
            num_scalar_prefetch=1,
            grid=(images,),
            in_specs=[
                pl.BlockSpec((1, length, width), lambda i, *_: (i, 0, 0)),
                pl.BlockSpec((1, length, 2), lambda i, *_: (first + i, 0, 0)),
                pl.BlockSpec(home.shape, lambda i, *_: (0, 0, 0)),
            ],
            out_specs=pl.BlockSpec((1, length, width), lambda i, *_: (i, 0, 0)),
        ),
        out_shape=jax.ShapeDtypeStruct((images, length, width), BF16),
        compiler_params=pltpu.CompilerParams(vmem_limit_bytes=VMEM_LIMIT),
        name="combine_output",
    )(count, hidden, slots_col, home)


ERF_P = 0.3275911
ERF_A = (0.254829592, -0.284496736, 1.421413741, -1.453152027, 1.061405429)


def gelu_pair(value):
    bell = jnp.exp(value * value * -0.5)
    ratio = 1.0 / (1.0 + jnp.abs(value) * (ERF_P / math.sqrt(2.0)))
    poly = ERF_A[4]
    for coefficient in ERF_A[3::-1]:
        poly = poly * ratio + coefficient
    tail = poly * ratio * bell * 0.5
    share = jnp.where(value < 0.0, tail, 1.0 - tail)
    return value * share, share + value * bell * (1.0 / math.sqrt(2.0 * math.pi))


def expert_kernel(
    place_ref, rows_ref, arrived_ref, router_ref, flat_ref, in_ref, out_ref, *refs, first, last, add,
):
    refs = list(refs)
    old_wide_ref = refs.pop(0) if add else None
    old_tall_ref = refs.pop(0) if add and last else None
    starts = None if first else (refs.pop(0), refs.pop(0))
    wide_ref = refs.pop(0)
    if last:
        result_ref, sent_ref, tall_ref = refs[:3]
        refs = refs[3:]
    forward_ref, backward_ref, left_s, thin_s, turned_s = refs
    step = pl.program_id(0)
    experts, padded, width = rows_ref.shape
    total = experts * padded
    wider = width + NARROW
    rows = rows_ref[...].reshape(total, width)
    delta = arrived_ref[:, :, :width].reshape(total, width)
    meta = arrived_ref[:, :, width:].reshape(total, LANES).astype(F32)
    lane_owner = lane_adapter((total, NARROW)).astype(F32)
    select = jnp.where(jnp.logical_and(lane_owner == meta[:, 0:1], meta[:, 2:3] > 0.5), 1.0, 0.0)

    def gates():
        lane = lax.broadcasted_iota(jnp.int32, (total, LANES), 1).astype(F32)
        own_expert = place_ref[1].astype(F32)
        is_own = (lane == own_expert).astype(F32)
        is_other = (lane == meta[:, 1:2]).astype(F32)
        logits = mm(rows, router_ref[...])
        own_logit = jnp.sum(logits * is_own, axis=-1, keepdims=True)
        other_logit = jnp.sum(logits * is_other, axis=-1, keepdims=True)
        peak = jnp.maximum(own_logit, other_logit)
        own_exp, other_exp = jnp.exp(own_logit - peak), jnp.exp(other_logit - peak)
        norm = 1.0 / (own_exp + other_exp)
        return own_exp * norm, other_exp * norm, is_own - is_other

    @pl.when(step == 0)
    def _():
        gate, _, _ = gates()
        grad_result = (delta.astype(F32) * gate).astype(BF16)
        thin_in = mm(rows, flat_ref[:, :NARROW]) * select
        grad_thin_out = mm(grad_result, flat_ref[:, NARROW:]) * select
        left_s[:, :width] = grad_result
        left_s[:, width:] = grad_thin_out.astype(BF16)
        thin_s[...] = thin_in.astype(BF16)
        turned_s[:NARROW, :] = thin_in.T.astype(BF16)
        turned_s[NARROW:, :] = grad_thin_out.T.astype(BF16)
        if first:
            forward_ref[...] = jnp.zeros_like(forward_ref)
            backward_ref[...] = jnp.zeros_like(backward_ref)
        else:
            forward_ref[...] = starts[0][...]
            backward_ref[...] = starts[1][...]

    up_in_t = out_ref[:, wider:]
    lifted = mm(rows, in_ref[...]) + mm_nt(thin_s[...], up_in_t)
    value, slope = gelu_pair(lifted)
    active = value.astype(BF16)
    grad_lifted = (mm_nt(left_s[...], out_ref[:, :wider]) * slope).astype(BF16)
    forward_ref[...] = forward_ref[...] + mm(active, out_ref[:, :wider])
    backward_ref[:, :width] = backward_ref[:, :width] + mm_nt(grad_lifted, in_ref[...])
    backward_ref[:, width:] = backward_ref[:, width:] + mm(grad_lifted, up_in_t)
    up_new = mm(turned_s[:NARROW, :], grad_lifted)
    down_new = mm(turned_s[NARROW:, :], active)
    if add:
        up_new = up_new + old_wide_ref[0, 0]
        down_new = down_new + old_wide_ref[0, 1]
    wide_ref[0, 0] = up_new.astype(wide_ref.dtype)
    wide_ref[0, 1] = down_new.astype(wide_ref.dtype)

    if last:
        @pl.when(step == pl.num_programs(0) - 1)
        def _():
            gate, other_gate, sides = gates()
            thin_out = (forward_ref[:, width:] * select).astype(BF16)
            grad_thin_in = (backward_ref[:, width:] * select).astype(BF16)
            result = (forward_ref[:, :width] + mm_nt(thin_out, flat_ref[:, NARROW:])).astype(BF16).astype(F32)
            down_in = mm_tn(grad_thin_in, rows)
            up_out = mm_tn(thin_out, left_s[:, :width])
            if add:
                down_in = down_in + old_tall_ref[:NARROW, :]
                up_out = up_out + old_tall_ref[NARROW:, :]
            tall_ref[:NARROW, :] = down_in.astype(tall_ref.dtype)
            tall_ref[NARROW:, :] = up_out.astype(tall_ref.dtype)
            result_ref[...] = (result * gate).astype(BF16).reshape(experts, padded, width)
            grad_gate = jnp.sum(delta.astype(F32) * result, axis=-1, keepdims=True)
            pull = sides * (gate * other_gate * grad_gate)
            high = pull.astype(BF16)
            rest = (pull - high.astype(F32)).astype(BF16)
            sent = backward_ref[:, :width] + mm_nt(grad_thin_in, flat_ref[:, :NARROW])
            sent = sent + (mm_nt(high, router_ref[...]) + mm_nt(rest, router_ref[...]))
            sent_ref[...] = sent.astype(BF16).reshape(experts, padded, width)


def expert_step(micro, place, rows, arrived, router, ins, first_ins, outs, parts, starts, last, old):
    experts, padded, width = rows.shape
    total = experts * padded
    hidden_units = outs.shape[0]
    piece = hidden_units // parts
    wider = width + NARROW
    flat_at = (first_ins.shape[1] - 2 * NARROW) // (2 * NARROW)
    kind = F32 if old is None else BF16
    wide = jax.ShapeDtypeStruct((parts, 2, NARROW, piece), kind)
    tall = jax.ShapeDtypeStruct((2 * NARROW, width), kind)
    sums = jax.ShapeDtypeStruct((total, wider), F32)
    whole = lambda array: pl.BlockSpec(array.shape, lambda i, *_: (0,) * len(array.shape))
    wide_block = pl.BlockSpec((1, 2, NARROW, piece), lambda i, *_: (i, 0, 0, 0))
    sent = jax.ShapeDtypeStruct((experts, padded, width), BF16)
    extra, extra_specs = [], []
    if old is not None:
        extra.append(old[0])
        extra_specs.append(wide_block)
        if last:
            extra.append(old[1])
            extra_specs.append(whole(old[1]))
    if starts is not None:
        extra += list(starts)
        extra_specs += [whole(array) for array in starts]
    if last:
        out_shape, out_specs = [wide, sent, sent, tall], [wide_block, whole(sent), whole(sent), whole(tall)]
        scratch = [pltpu.VMEM((total, wider), F32), pltpu.VMEM((total, wider), F32)]
    else:
        out_shape, out_specs, scratch = [wide, sums, sums], [wide_block, whole(sums), whole(sums)], []
    scratch += [
        pltpu.VMEM((total, wider), BF16),
        pltpu.VMEM((total, NARROW), BF16),
        pltpu.VMEM((2 * NARROW, total), BF16),
    ]
    return pl.pallas_call(
        functools.partial(expert_kernel, first=starts is None, last=last, add=old is not None),
        grid_spec=pltpu.PrefetchScalarGridSpec(
            num_scalar_prefetch=1,
            grid=(parts,),
            in_specs=[
                whole(rows),
                pl.BlockSpec((experts, padded, width + LANES), lambda i, *_: (0, micro, 0)),
                whole(router),
                pl.BlockSpec((width, 2 * NARROW), lambda i, *_: (0, flat_at)),
                pl.BlockSpec((width, piece), lambda i, *_: (0, i)),
                pl.BlockSpec((piece, wider + NARROW), lambda i, *_: (i, 0)),
            ]
            + extra_specs,
            out_specs=out_specs,
            scratch_shapes=scratch,
        ),
        out_shape=out_shape,
        compiler_params=pltpu.CompilerParams(vmem_limit_bytes=VMEM_LIMIT),
        cost_estimate=cost(8 * total * width * hidden_units, 2),
        name="expert_step",
    )(place, rows, arrived, router, first_ins, ins, outs, *extra)


def line_gather(array, size):
    down, up = [], []
    moving = array
    for step in range(1, size):
        moving = lax.ppermute(moving, "dp", [(i, i - 1) for i in range(1, size - step + 1)])
        down.append(moving)
    moving = array
    for step in range(1, size):
        moving = lax.ppermute(moving, "dp", [(i, i + 1) for i in range(step - 1, size - 1)])
        up.append(moving)
    return [array] + down + up


def line_stack(pieces, size):
    place = lax.axis_index("dp")
    ordered = []
    for part in range(size):
        chosen = None
        for holder in range(size):
            which = 0 if part == holder else (part - holder if part > holder else size - 1 + holder - part)
            chosen = pieces[which] if chosen is None else jnp.where(place == holder, pieces[which], chosen)
        ordered.append(chosen)
    return jnp.stack(ordered)


def line_scatter(own, size):
    place = lax.axis_index("dp")
    pick = lambda index: lax.dynamic_index_in_dim(own, jnp.clip(index, 0, size - 1), 0, keepdims=False)
    total = pick(place).astype(F32)
    for sign in (1, -1):
        arriving = None
        for step in range(1, size):
            message = pick(place + sign * (size - step))
            if arriving is not None:
                message = (message.astype(F32) + arriving.astype(F32)).astype(BF16)
            edges = [(i, i + 1) if sign > 0 else (size - 1 - i, size - 2 - i) for i in range(step)]
            arriving = lax.ppermute(message, "dp", edges)
        total = total + arriving.astype(F32)
    return total


def swap(array, bit, size):
    return lax.ppermute(array, "expert", [(i, i ^ bit) for i in range(size)])


def dense_gather(packed, half, size_dp, size_expert, ahead):
    rows = packed.shape[0]
    if size_expert < 4 or size_expert & (size_expert - 1) or (2 * rows) % 8:
        full = lax.all_gather(packed, ("dp", "expert"), axis=0, tiled=True)
        return full[:, :half], full[:, half:]
    place = lax.axis_index("expert")
    core = place % 2
    low, high = packed[:, :half], packed[:, half:]
    kept = jnp.where(core == 0, low, high)
    other = swap(jnp.where(core == 0, high, low), 1, size_expert)
    pair = jnp.concatenate([jnp.where(core == 0, kept, other), jnp.where(core == 0, other, kept)], axis=0)
    pieces = line_gather(pair, size_dp)
    stacked, _ = lax.optimization_barrier((line_stack(pieces, size_dp), ahead))
    bits = [1 << b for b in range(1, size_expert.bit_length() - 1)]
    cut = (half // LANES + 1) // 2 * LANES
    done = []
    for stream, order in ((stacked[:, :, :cut], bits), (stacked[:, :, cut:], bits[::-1])):
        held = []
        for bit in order:
            axis = 1 + sum(1 for other_bit in held if other_bit > bit)
            arrived = swap(stream, bit, size_expert)
            mine = (place // bit) % 2 == 0
            stream = jnp.stack([jnp.where(mine, stream, arrived), jnp.where(mine, arrived, stream)], axis=axis)
            held.append(bit)
        done.append(stream.reshape(-1, stream.shape[-1]))
    side = jnp.concatenate(done, axis=1)
    arrived = swap(side, 1, size_expert)
    return jnp.where(core == 0, side, arrived), jnp.where(core == 0, arrived, side)


def full_scatter(own, size_dp, size_expert):
    rows = own.shape[0] // (size_dp * size_expert)
    if size_expert < 4 or size_expert & (size_expert - 1) or rows % 8:
        return lax.psum_scatter(own.astype(F32), ("dp", "expert"), scatter_dimension=0, tiled=True)
    place = lax.axis_index("expert")
    columns = own.shape[1]
    bits = [1 << b for b in range(1, size_expert.bit_length() - 1)]

    def halve(array, axis, bit):
        side = (place // bit) % 2
        mine = lax.dynamic_index_in_dim(array, side, axis, keepdims=False)
        other = lax.dynamic_index_in_dim(array, 1 - side, axis, keepdims=False)
        return (mine.astype(F32) + swap(other, bit, size_expert).astype(F32)).astype(BF16)

    grid = own.reshape((size_dp,) + (2,) * (len(bits) + 1) + (rows, columns))
    grid = halve(grid, len(bits) + 1, 1)
    cut = (columns // LANES + 1) // 2 * LANES
    done = []
    for stream, order in ((grid[..., :cut], bits), (grid[..., cut:], bits[::-1])):
        left = list(bits[::-1])
        for bit in order:
            stream = halve(stream, 1 + left.index(bit), bit)
            left.remove(bit)
        done.append(stream)
    return line_scatter(jnp.concatenate(done, axis=-1), size_dp)


def exchange(array):
    return lax.all_to_all(array, "expert", split_axis=0, concat_axis=0, tiled=True)


def shards(
    tokens, image_count, adapter_index, expert_ids, norm_gains, attention_in, attention_out, router,
    expert_in, expert_out, attention_down, attention_up, expert_down_in, expert_up_in,
    expert_down_out, expert_up_out, cotangent,
):
    micros, images, length, width = tokens.shape
    size_dp = lax.axis_size("dp")
    experts = lax.axis_size("expert")
    hidden_units = expert_in.shape[2]
    rows = images * length
    capacity = capacity_of(rows, experts)
    padded = -(-capacity // 16) * 16
    shard_rows = attention_in.shape[0]

    piece, shard = hidden_units // size_dp, width // size_dp
    chunks = 2 if piece % (2 * LANES) == 0 else 1
    part = piece // chunks
    by_shard = expert_in[0].reshape(shard, size_dp, piece)
    sides = jnp.concatenate(
        [expert_down_in[0].reshape(shard, NARROW), expert_up_out[0].reshape(NARROW, shard).T], axis=1
    )
    beside = jnp.concatenate(
        [expert_out[0], expert_down_out[0].reshape(piece, NARROW), expert_up_in[0].reshape(NARROW, piece).T], axis=1
    )
    weights = []
    for chunk in range(chunks):
        own_in = by_shard[:, :, chunk * part : (chunk + 1) * part].reshape(shard, size_dp * part)
        own_out = beside[chunk * part : (chunk + 1) * part]
        if chunk == 0:
            own_in = jnp.concatenate([own_in, sides], axis=1)
        weights.append(
            (
                lax.all_gather(own_in, "dp", axis=0, tiled=True),
                lax.all_gather(own_out, "dp", axis=0, tiled=True),
            )
        )

    picks = expert_ids.reshape(micros, 2 * rows)
    hits = (picks[:, :, None] == jnp.arange(experts, dtype=jnp.int32)).astype(jnp.int32)
    placed = jnp.sum((jnp.cumsum(hits, axis=1) - 1) * hits, axis=2)
    slots_col = (picks * padded + placed).reshape(micros * images, length, 2)
    slots_row = jnp.swapaxes(slots_col, 1, 2)
    ids4 = expert_ids.reshape(micros * images, length, 2)
    lane = jnp.arange(LANES, dtype=jnp.int32)
    adapt4 = adapter_index.reshape(micros * images)
    other = jnp.swapaxes(ids4[:, :, ::-1], 1, 2)[..., None]
    meta = jnp.where(
        lane == 0,
        adapt4[:, None, None, None],
        jnp.where(lane == 1, other, jnp.where(lane == 2, 1, 0)),
    ).astype(BF16)
    x4 = tokens.reshape(micros * images, length, width)
    cot4 = cotangent.reshape(micros * images, length, width)
    counts = image_count.reshape(micros)
    sent_delta = dispatch(counts, cot4, slots_row, meta, experts, padded)
    arrived = exchange(sent_delta)

    half = 2 * width + 4 * NARROW + LANES
    small = jnp.concatenate([router, norm_gains.T], axis=1)
    small = jnp.pad(small, ((0, 0), (0, LANES - small.shape[1])))
    packed = jnp.concatenate(
        [
            attention_in[:, : 2 * width],
            attention_down.reshape(shard_rows, 4 * NARROW),
            small,
            attention_in[:, 2 * width :],
            attention_out,
            attention_up.reshape(4 * NARROW, shard_rows).T,
            jnp.zeros((shard_rows, LANES), BF16),
        ],
        axis=1,
    )
    side_a, side_b = dense_gather(packed, half, size_dp, experts, sent_delta)
    tail = side_a[:, 2 * width + 4 * NARROW :]
    gains = tail[:, experts : experts + 2].astype(F32).T
    router_full = jnp.where(jnp.arange(LANES)[None, :] < experts, tail, jnp.zeros_like(tail))

    place = jnp.stack([lax.axis_index("dp"), lax.axis_index("expert")]).astype(jnp.int32)
    kept, received = [], []
    for micro in range(micros):
        adapt = adapter_index[micro]
        if kept:
            adapt, _ = lax.optimization_barrier((adapt, kept[-1][3]))
        *saved, sent = attention_forward(micro, adapt, x4, side_a, side_b, gains, slots_row, experts, padded)
        kept.append(saved)
        received.append(exchange(sent))
    step = functools.partial(expert_step, place=place, arrived=arrived, router=router_full, parts=size_dp)
    sums, old = [None] * micros, [None] * chunks
    results, backs = [], []
    for chunk in range(chunks):
        last = chunk == chunks - 1
        if chunk:
            step = functools.partial(step, place=lax.optimization_barrier((place, sums[-1][0]))[0])
        for micro in range(micros):
            new_wide, *rest = step(
                micro, rows=received[micro], ins=weights[chunk][0], first_ins=weights[0][0],
                outs=weights[chunk][1], starts=sums[micro], last=last, old=old[chunk],
            )
            old[chunk] = (new_wide, rest[2]) if last else (new_wide, None)
            if last:
                results.append(rest[0])
                back = rest[1]
                if backs:
                    back, backs[-1] = lax.optimization_barrier((back, backs[-1]))
                backs.append(exchange(back))
            else:
                sums[micro] = tuple(rest)
    outputs, input_grads, dense_own = [], [], None
    for micro in range(micros):
        input_grad, dense_own = attention_backward(
            micro, adapter_index[micro], image_count[micro], x4, cot4, side_a, side_b, gains,
            slots_col, kept[micro], backs[micro], dense_own, micro == micros - 1,
        )
        input_grads.append(input_grad)
    ahead = backs[-1]
    for micro in range(micros):
        result, _ = lax.optimization_barrier((results[micro], ahead))
        ahead = exchange(result)
        outputs.append(combine_output(micro, image_count[micro], kept[micro][4], slots_col, ahead))

    wide = jnp.concatenate([entry[0] for entry in old], axis=3).reshape(size_dp, 2 * NARROW, piece)
    tall = jnp.swapaxes(old[-1][1].reshape(2 * NARROW, size_dp, shard), 0, 1)
    sparse = line_scatter(jnp.concatenate([wide, tall], axis=2).astype(BF16), size_dp)
    wide = sparse[:, :piece].reshape(2, NARROW, piece)
    tall = sparse[:, piece:]
    dense = full_scatter(dense_own.astype(BF16), size_dp, experts)
    return (
        jnp.stack(outputs),
        jnp.stack(input_grads),
        dense[:, : 4 * NARROW].reshape(shard_rows, 4, ADAPTERS, RANK),
        dense[:, 4 * NARROW :].T.reshape(4, ADAPTERS, RANK, shard_rows),
        tall[:NARROW].T.reshape(1, shard, ADAPTERS, RANK),
        wide[0].reshape(1, ADAPTERS, RANK, piece),
        wide[1].T.reshape(1, piece, ADAPTERS, RANK),
        tall[NARROW:].reshape(1, ADAPTERS, RANK, shard),
    )


def solution(mesh):
    everywhere = ("dp", "expert")
    return jax.shard_map(
        shards,
        mesh=mesh,
        in_specs=(
            P(None, everywhere, None, None),
            P(None, everywhere),
            P(None, everywhere),
            P(None, everywhere, None, None),
            P(None, everywhere),
            P(everywhere, None),
            P(everywhere, None),
            P(everywhere, None),
            P("expert", "dp", None),
            P("expert", "dp", None),
            P(everywhere, None, None, None),
            P(None, None, None, everywhere),
            P("expert", "dp", None, None),
            P("expert", None, None, "dp"),
            P("expert", "dp", None, None),
            P("expert", None, None, "dp"),
            P(None, everywhere, None, None),
        ),
        out_specs=(
            P(None, everywhere, None, None),
            P(None, everywhere, None, None),
            P(everywhere, None, None, None),
            P(None, None, None, everywhere),
            P("expert", "dp", None, None),
            P("expert", None, None, "dp"),
            P("expert", "dp", None, None),
            P("expert", None, None, "dp"),
        ),
        check_vma=False,
    )
```
